32 devices in a mesh: pheno: 2 (over x), samp: 8 (over z, y), var: 2 (over core).
Axes of the slice: x: 2, y: 2, z: 4, core: 2. Of those that a mesh axis runs over, the one named last changes fastest.
Arguments:
- genotypes: bfloat16 [4608, 16384], P('samp', 'var'), may hold values from -6 to 6, as said below
- coefficients: float32 [64, 16384], P('pheno', 'var'), parts along dimension 0, may hold values from -0.5 to 0.5
- time_order: int32 [9216], P(('pheno', 'samp')), parts along dimension 0, may hold values from 0 to 4607, as said below
- fold_label: int32 [9216], P(('pheno', 'samp')), parts along dimension 0, may hold values from 0 to 7
- event_flag: int32 [9216], P(('pheno', 'samp')), parts along dimension 0, may hold values 0 or 1
- penalty: float32 [32], replicated, may hold values from 0.3 to 1.5
- step_size: float32 [32], replicated, may hold values from 0.2 to 1
Outputs:
- coefficients_out: float32 [64, 16384], P('pheno', 'var'), parts along dimension 0
- score: bfloat16 [64, 4608], P('pheno', 'samp'), parts along dimension 0
The draws below stay inside these ranges and needn't reach their ends.
There are 2 independent parts, one for each index of `pheno`. The reference program is written for one: setup_inputs(seed, part) draws one part's arguments, and reference() takes and returns one part's arrays. A program takes and returns all parts, laid end to end along the dimension named above; an argument that names none is the same for every part. Nothing has to cross between parts.
Inputs may be any that keep to these rules, and one draw needn't show every extreme that they name: time_order names every sample ID once; each block of 576 consecutive IDs holds exactly 576 / 8 of the IDs in each block of 576 consecutive time ranks. `genotypes`: entries of mean zero and unit variance.
All inputs are finite; a program needn't handle non-finite values. No bound on the sum of `event_flag` on one device may be relied on, other than what follows from the above.
Results may differ from the reference program's by a relative error of at most 0.0027.
Values may be sent and summed in bfloat16 or wider, within the bound.
A program may use at most 64 MiB of HBM per device.

```python
import math
import jax
import jax.numpy as jnp
from jax import lax

S_DEV = 576
VARS = 16384
COLS = 32
FOLDS = 8
ITERS = 3
SAMPLES = 4608
N_SAMP = 8


def draw_time_order(key, part):
    share = S_DEV // N_SAMP
    first_key = jax.random.fold_in(key, 11)
    second_key = jax.random.fold_in(key, 23)
    identity = jnp.arange(SAMPLES, dtype=jnp.int32).reshape(N_SAMP, S_DEV)
    row_keys = jax.random.split(first_key, N_SAMP)
    mixed = jax.vmap(lambda one_key, row: jax.random.permutation(one_key, row))(row_keys, identity)
    grouped = mixed.reshape(N_SAMP, N_SAMP, share).transpose(1, 0, 2).reshape(N_SAMP, S_DEV)
    block_keys = jax.random.split(second_key, N_SAMP)
    ranked = jax.vmap(lambda one_key, row: jax.random.permutation(one_key, row))(block_keys, grouped)
    return ranked.reshape(SAMPLES).astype(jnp.int32)


def draw_genotypes(key, part):
    own_key = jax.random.fold_in(key, 37)
    values = jnp.clip(jax.random.normal(own_key, (SAMPLES, VARS), jnp.float32), -6.0, 6.0)
    return values.astype(jnp.bfloat16)


def with_ends(drawn, stream_key, smallest, largest):
    longest = drawn.shape.index(max(drawn.shape))
    spots = []
    for shift in (0, 1):
        where = [jax.random.randint(jax.random.fold_in(stream_key, axis), (), 0, length) for axis, length in enumerate(drawn.shape)]
        where[longest] = (where[longest] + shift) % drawn.shape[longest]
        spots.append(tuple(where))
    return drawn.at[spots[0]].set(smallest).at[spots[1]].set(largest)


def block_levels(key, extent, cuts, low, largest):
    def one(dim, parts):
        draws = jax.random.uniform(jax.random.fold_in(jax.random.fold_in(key, 6), dim), (parts,), jnp.float32, low / len(cuts), largest / len(cuts))
        return jnp.repeat(jnp.exp(draws), extent[dim] // parts).reshape((-1,) + (1,) * (len(extent) - dim - 1))

    gain = one(*cuts[0])
    for cut in cuts[1:]:
        gain = gain * one(*cut)
    return gain


def setup_inputs(seed: int = 0, part: int = 0) -> dict:
    seeds = jax.random.split(jax.random.key(seed), 8)
    own_keys = jax.random.split(jax.random.fold_in(seeds[7], part), 8)
    return {
        "genotypes": draw_genotypes(jax.random.fold_in(seeds[7], 71), part),
        "coefficients": jnp.clip(jax.random.uniform(own_keys[1], (COLS, VARS), jnp.float32, -0.5, 0.5) * block_levels(own_keys[1], (COLS, VARS), ((1, 2),), -0.4, 0.0), -0.5, 0.5),
        "time_order": draw_time_order(jax.random.fold_in(jax.random.fold_in(seeds[7], part), 71), part),
        "fold_label": with_ends(jax.random.randint(own_keys[3], (SAMPLES,), 0, FOLDS), jax.random.fold_in(own_keys[3], 1), 0, FOLDS - 1).astype(jnp.int32),
        "event_flag": with_ends((jax.random.randint(own_keys[4], (SAMPLES,), 0, 3) < 1).astype(jnp.int32), jax.random.fold_in(own_keys[4], 1), 0, 1),
        "penalty": jnp.clip(jnp.exp(jax.random.uniform(seeds[5], (COLS,), jnp.float32, math.log(0.3), math.log(1.5))), 0.3, 1.5),
        "step_size": jnp.clip(jnp.exp(jax.random.uniform(seeds[6], (COLS,), jnp.float32, math.log(0.2), math.log(1.0))), 0.2, 1.0),
    }


def shrink(coef, gradient, penalty, step_size):
    stepped = coef - step_size[:, None] * gradient
    threshold = (step_size * penalty)[:, None]
    return jnp.sign(stepped) * jnp.maximum(jnp.abs(stepped) - threshold, 0.0)

def reference(genotypes, coefficients, time_order, fold_label, event_flag, penalty, step_size):
    column_fold = jnp.arange(COLS, dtype=jnp.int32) % FOLDS
    fold_time = fold_label[time_order]
    event_time = event_flag[time_order].astype(jnp.float32)
    train_mask = (fold_time[None, :] != column_fold[:, None]).astype(jnp.float32)
    events_kept = train_mask * event_time[None, :]
    coef = coefficients
    score_low = jnp.zeros((COLS, SAMPLES), jnp.bfloat16)
    for step in range(ITERS):
        coef_low = coef.astype(jnp.bfloat16)
        predictor = lax.dot_general(coef_low, genotypes, (((1,), (1,)), ((), ())), preferred_element_type=jnp.float32)
        predictor = predictor * (1.0 / math.sqrt(VARS))
        weight = train_mask * jnp.exp(predictor[:, time_order])
        risk = lax.cumsum(weight, axis=1, reverse=True)
        ratio = events_kept / jnp.where(events_kept > 0, risk, 1.0)
        hazard = lax.cumsum(ratio, axis=1)
        score_time = (weight * hazard - events_kept).astype(jnp.bfloat16)
        score_low = jnp.zeros((COLS, SAMPLES), jnp.bfloat16).at[:, time_order].set(score_time)
        gradient = jnp.dot(score_low, genotypes, preferred_element_type=jnp.float32) * (1.0 / math.sqrt(SAMPLES))
        coef = shrink(coef, gradient, penalty, step_size)
    return (coef, score_low)
```

```python
import functools
import math

import jax
import jax.numpy as jnp
from jax import lax
from jax.experimental import pallas as pl
from jax.experimental.pallas import tpu as pltpu
from jax.sharding import PartitionSpec as P

VARS = 16384
FOLDS = 8
ITERS = 3
MESH = pl.DeviceIdType.MESH
F32 = jnp.float32
BF16 = jnp.bfloat16


def each(count, body):
    if count <= 8:
        for step in range(count):
            body(step)
    else:
        lax.fori_loop(0, count, lambda step, carry: (body(step), carry)[1], 0)


def halves(value):
    high = value.astype(BF16)
    low = (value - high.astype(F32)).astype(BF16)
    return jnp.concatenate([high, low], axis=0)


def dot2(value, matrix):
    rows = value.shape[0]
    both = jnp.dot(halves(value), matrix, preferred_element_type=F32)
    return both[:rows] + both[rows:]


def path_kernel(
    count, scale_vars, scale_samples,
    geno, coef_in, to_time, later, earlier, to_id, mask, kept, kept_time, step_size, penalty,
    coef_out, score_out,
    low, shard, half_send, half_recv, out_a, in_a, out_b, in_b, out_g, in_g, pred,
    half_ss, half_rs, a_ss, a_rs, b_ss, b_rs, g_ss, g_rs, c_ss, c_rs, f_ss, f_rs,
):
    me = lax.axis_index("samp")
    var = lax.axis_index("var")
    columns, variants = coef_in.shape
    rows = geno.shape[0]
    part = variants // count
    width = later.shape[0] // count

    def peer(step):
        return lax.rem(me + step, count)

    def piece(owner):
        return pl.ds(pl.multiple_of(owner * part, part), part)

    def slots(owner):
        return pl.ds(pl.multiple_of(owner * width, width), width)

    barrier = pltpu.get_barrier_semaphore()

    def greet(step):
        pl.semaphore_signal(barrier, inc=1, device_id={"samp": peer(step + 1)}, device_id_type=MESH)

    each(count - 1, greet)
    pl.semaphore_signal(barrier, inc=1, device_id={"var": 1 - var}, device_id_type=MESH)
    pl.semaphore_wait(barrier, count)

    def send(source, target, ssem, rsem, owner):
        return pltpu.make_async_remote_copy(
            src_ref=source,
            dst_ref=target,
            send_sem=ssem.at[owner],
            recv_sem=rsem.at[me],
            device_id={"samp": owner},
            device_id_type=MESH,
        )

    def arrive(source, target, ssem, rsem, owner):
        pltpu.make_async_remote_copy(
            src_ref=source,
            dst_ref=target,
            send_sem=ssem.at[owner],
            recv_sem=rsem.at[owner],
            device_id={"samp": owner},
            device_id_type=MESH,
        ).wait_recv()

    def fill(step):
        low[step] = coef_in[:, piece(step)].astype(BF16)

    each(count, fill)
    shard[...] = coef_in[:, piece(me)]

    def one_step(turn, carry):
        pred[...] = jnp.zeros_like(pred)

        def add_part(step):
            owner = peer(step)
            if not (isinstance(step, int) and step == 0):
                @pl.when(turn > 0)
                def _():
                    if isinstance(step, int):
                        arrive(low.at[owner], low.at[owner], c_ss, c_rs, owner)
                    else:
                        @pl.when(step > 0)
                        def _():
                            arrive(low.at[owner], low.at[owner], c_ss, c_rs, owner)
            pred[...] += lax.dot_general(
                low[owner], geno[:, piece(owner)], (((1,), (1,)), ((), ())), preferred_element_type=F32
            )

        each(count, add_part)
        half_send[...] = pred[...]
        slot = lax.rem(turn, 2)
        swap = pltpu.make_async_remote_copy(
            src_ref=half_send, dst_ref=half_recv.at[slot], send_sem=half_ss, recv_sem=half_rs.at[slot],
            device_id={"var": 1 - var}, device_id_type=MESH,
        )
        swap.start()
        swap.wait()

        @pl.when(turn > 0)
        def _():
            def drained(step):
                owner = peer(step + 1)
                send(low.at[me], low.at[me], c_ss, c_rs, owner).wait_send()
            each(count - 1, drained)

        weight = mask[...] * jnp.exp((half_send[...] + half_recv[slot]) * scale_vars)
        pred[...] = weight
        spread = dot2(weight, to_time[...])
        for owner in range(count):
            out_a[owner] = spread[:, owner * width:(owner + 1) * width]

        def push_a(step):
            owner = peer(step + 1)
            send(out_a.at[owner], in_a.at[me], a_ss, a_rs, owner).start()
        each(count - 1, push_a)
        risk = dot2(out_a[me], later[slots(me), :])
        for step in range(count - 1):
            owner = peer(step + 1)
            arrive(out_a.at[owner], in_a.at[owner], a_ss, a_rs, owner)
            risk += dot2(in_a[owner], later[slots(owner), :])
        events = kept_time[...]
        ratio = events / jnp.where(events > 0, risk, 1.0)
        spread = dot2(ratio, earlier[...])
        for owner in range(count):
            out_b[owner] = spread[:, owner * width:(owner + 1) * width]

        def push_b(step):
            owner = peer(step + 1)
            send(out_b.at[owner], in_b.at[me], b_ss, b_rs, owner).start()
        each(count - 1, push_b)
        hazard = dot2(out_b[me], to_id[slots(me), :])
        for step in range(count - 1):
            owner = peer(step + 1)
            arrive(out_b.at[owner], in_b.at[owner], b_ss, b_rs, owner)
            hazard += dot2(in_b[owner], to_id[slots(owner), :])
        score_out[...] = (pred[...] * hazard - kept[...]).astype(BF16)

        def push_g(step):
            owner = peer(step + 1)
            out_g[owner] = jnp.dot(
                score_out[...], geno[:, piece(owner)], preferred_element_type=F32
            ).astype(out_g.dtype)
            send(out_g.at[owner], in_g.at[me], g_ss, g_rs, owner).start()
        each(count - 1, push_g)
        total = jnp.dot(score_out[...], geno[:, piece(me)], preferred_element_type=F32)
        for step in range(count - 1):
            owner = peer(count - 1 - step)
            arrive(out_g.at[owner], in_g.at[owner], g_ss, g_rs, owner)
            total += in_g[owner].astype(F32)
        pace = step_size[...]
        stepped = shard[...] - pace * (total * scale_samples)
        shrunk = jnp.maximum(jnp.abs(stepped) - pace * penalty[...], 0.0)
        fresh = jnp.where(stepped > 0, shrunk, -shrunk)
        shard[...] = fresh

        def drained_all(step):
            owner = peer(step + 1)
            send(out_a.at[owner], in_a.at[me], a_ss, a_rs, owner).wait_send()
            send(out_b.at[owner], in_b.at[me], b_ss, b_rs, owner).wait_send()
            send(out_g.at[owner], in_g.at[me], g_ss, g_rs, owner).wait_send()

        @pl.when(turn < ITERS - 1)
        def _():
            low[me] = fresh.astype(BF16)

            def push_c(step):
                owner = peer(step + 1)
                send(low.at[me], low.at[me], c_ss, c_rs, owner).start()
            each(count - 1, push_c)

        each(count - 1, drained_all)
        return carry

    lax.fori_loop(0, ITERS, one_step, 0)

    coef_out[:, piece(me)] = shard[...]

    def push_f(step):
        owner = peer(step + 1)
        send(shard, coef_out.at[:, piece(me)], f_ss, f_rs, owner).start()
    each(count - 1, push_f)

    def land_f(step):
        owner = peer(step + 1)
        arrive(shard, coef_out.at[:, piece(owner)], f_ss, f_rs, owner)
        send(shard, coef_out.at[:, piece(me)], f_ss, f_rs, owner).wait_send()
    each(count - 1, land_f)


def local(genotypes, coefficients, time_order, fold_label, event_flag, penalty, step_size):
    rows = genotypes.shape[0]
    columns, variants = coefficients.shape
    count = lax.axis_size("samp")
    me = lax.axis_index("samp")
    share = rows // count
    width = -(-(share + count) // 128) * 128
    total = count * width
    part = variants // count

    ranks = jnp.arange(rows, dtype=jnp.int32)
    slot_all = jnp.arange(total, dtype=jnp.int32)
    lane = slot_all % width
    group = slot_all // width
    owner = time_order // rows
    place = time_order % rows
    same = (owner[:, None] == owner[None, :]) & (ranks[:, None] < ranks[None, :])
    key = owner * width + jnp.sum(same.astype(jnp.int32), axis=0)
    match = key[:, None] == slot_all[None, :]
    rank_of = jnp.max(jnp.where(match, ranks[:, None], -1), axis=0)
    place_of = jnp.max(jnp.where(match, place[:, None], -1), axis=0)
    place_in = lax.all_to_all(place_of.reshape(count, width), "samp", 0, 0, tiled=True).reshape(total)
    match_id = place_in[None, :] == ranks[:, None]
    code = fold_label * 2 + event_flag
    code_out = jnp.sum(jnp.where(match_id, code[:, None], 0), axis=0)
    code_in = lax.all_to_all(code_out.reshape(count, width), "samp", 0, 0, tiled=True).reshape(total)
    code_time = jnp.sum(jnp.where(rank_of[None, :] == ranks[:, None], code_in[None, :], 0), axis=1)
    block = jnp.sum(jnp.where(match_id, group[None, :], 0), axis=1)

    in_totals = (lane >= share) & (lane < share + count)
    to_time = (match_id | (in_totals[None, :] & ((lane - share)[None, :] == block[:, None]))).astype(BF16)
    reach = jnp.where(lane < share, rank_of, jnp.where(in_totals & (lane - share > me), rows, -1))
    later = (reach[:, None] >= ranks[None, :]).astype(BF16)
    back = jnp.where(lane < share, rank_of, jnp.where(lane == share, rows, -1))
    earlier = (ranks[:, None] <= back[None, :]).astype(BF16)
    to_id = (
        (place_in[:, None] == ranks[None, :])
        | ((lane == share)[:, None] & (group[:, None] < block[None, :]))
    ).astype(BF16)

    column_fold = jnp.arange(columns, dtype=jnp.int32) % FOLDS
    mask = (fold_label[None, :] != column_fold[:, None]).astype(F32)
    kept = mask * event_flag.astype(F32)[None, :]
    kept_time = ((code_time // 2)[None, :] != column_fold[:, None]).astype(F32) * (code_time % 2).astype(F32)[None, :]

    vmem = pl.BlockSpec(memory_space=pltpu.VMEM)
    dma = pltpu.SemaphoreType.DMA
    return pl.pallas_call(
        functools.partial(path_kernel, count, 1.0 / math.sqrt(VARS), 1.0 / math.sqrt(rows * count)),
        out_shape=(
            jax.ShapeDtypeStruct((columns, variants), F32),
            jax.ShapeDtypeStruct((columns, rows), BF16),
        ),
        in_specs=[vmem] * 11,
        out_specs=(vmem, vmem),
        scratch_shapes=[
            pltpu.VMEM((count, columns, part), BF16),
            pltpu.VMEM((columns, part), F32),
            pltpu.VMEM((columns, rows), F32),
            pltpu.VMEM((2, columns, rows), F32),
            pltpu.VMEM((count, columns, width), F32),
            pltpu.VMEM((count, columns, width), F32),
            pltpu.VMEM((count, columns, width), F32),
            pltpu.VMEM((count, columns, width), F32),
            pltpu.VMEM((count, columns, part), BF16),
            pltpu.VMEM((count, columns, part), BF16),
            pltpu.VMEM((columns, rows), F32),
            dma, dma((2,)),
        ] + [dma((count,))] * 10,
        compiler_params=pltpu.CompilerParams(
            collective_id=0, has_side_effects=True, vmem_limit_bytes=60 * 1024 * 1024
        ),
    )(
        genotypes, coefficients, to_time, later, earlier, to_id, mask, kept, kept_time,
        step_size[:, None], penalty[:, None],
    )


def solution(mesh):
    placed = (
        P("samp", "var"),
        P("pheno", "var"),
        P(("pheno", "samp")),
        P(("pheno", "samp")),
        P(("pheno", "samp")),
        P(),
        P(),
    )
    return jax.shard_map(
        local,
        mesh=mesh,
        in_specs=placed,
        out_specs=(P("pheno", "var"), P("pheno", "samp")),
        check_vma=False,
    )
```

```python
import functools
import math

import jax
import jax.numpy as jnp
from jax import lax
from jax.experimental import pallas as pl
from jax.experimental.pallas import tpu as pltpu
from jax.sharding import PartitionSpec as P

VARS = 16384
FOLDS = 8
ITERS = 3
MESH = pl.DeviceIdType.MESH
F32 = jnp.float32
BF16 = jnp.bfloat16


def each(count, body):
    if count <= 8:
        for step in range(count):
            body(step)
    else:
        lax.fori_loop(0, count, lambda step, carry: (body(step), carry)[1], 0)


def halves(value):
    high = value.astype(BF16)
    low = (value - high.astype(F32)).astype(BF16)
    return jnp.concatenate([high, low], axis=0)


def across(left, right):
    return lax.dot_general(left, right, (((1,), (1,)), ((), ())), preferred_element_type=F32)


def across2(value, matrix):
    rows = value.shape[0]
    both = across(halves(value), matrix)
    return both[:rows] + both[rows:]


def dot2(value, matrix):
    rows = value.shape[0]
    both = jnp.dot(halves(value), matrix, preferred_element_type=F32)
    return both[:rows] + both[rows:]


def path_kernel(
    count, scale_vars, scale_samples,
    geno_in, coef_in, labels, place_out, reach, back, spot, step_size, penalty,
    coef_out, score_out,
    geno, to_time, later, earlier, to_id, mask, kept, kept_time, place_in, code_out, code_in,
    low, shard, half_send, half_recv, out_a, in_a, out_b, in_b, out_g, in_g, pred,
    load_sem, p_ss, p_rs, l_ss, l_rs, fwd_ss, last_ss, half_ss, half_rs, a_ss, a_rs, b_ss, b_rs, g_ss, g_rs, c_ss, c_rs, f_ss, f_rs,
):
    me = lax.axis_index("samp")
    var = lax.axis_index("var")
    columns, variants = coef_in.shape
    rows = geno.shape[0]
    part = variants // count
    width = later.shape[1] // count
    share = rows // count
    half = count // 2
    load = pltpu.make_async_copy(geno_in, geno, load_sem)
    load.start()

    def peer(step):
        return lax.rem(me + step, count)

    def piece(owner):
        return pl.ds(pl.multiple_of(owner * part, part), part)

    side = 1 - 2 * lax.rem(me, 2)

    def down(step):
        return lax.rem(me + 2 * step, count)

    def slots(owner):
        return pl.ds(pl.multiple_of(owner * width, width), width)

    barrier = pltpu.get_barrier_semaphore()

    def greet(step):
        pl.semaphore_signal(barrier, inc=1, device_id={"samp": peer(step + 1)}, device_id_type=MESH)

    each(count - 1, greet)
    pl.semaphore_signal(barrier, inc=1, device_id={"var": 1 - var}, device_id_type=MESH)
    pl.semaphore_wait(barrier, count)

    def send(source, target, ssem, rsem, owner):
        return pltpu.make_async_remote_copy(
            src_ref=source,
            dst_ref=target,
            send_sem=ssem.at[owner],
            recv_sem=rsem.at[me],
            device_id={"samp": owner},
            device_id_type=MESH,
        )

    def relay(source, target, ssem, rsem, owner):
        return pltpu.make_async_remote_copy(
            src_ref=source,
            dst_ref=target,
            send_sem=ssem.at[owner],
            recv_sem=rsem.at[owner],
            device_id={"samp": me + side},
            device_id_type=MESH,
        )

    def arrive(source, target, ssem, rsem, owner):
        pltpu.make_async_remote_copy(
            src_ref=source,
            dst_ref=target,
            send_sem=ssem.at[owner],
            recv_sem=rsem.at[owner],
            device_id={"samp": owner},
            device_id_type=MESH,
        ).wait_recv()

    def push_p(step):
        owner = peer(step + 1)
        send(place_out.at[owner], place_in.at[me], p_ss, p_rs, owner).start()
    each(count - 1, push_p)

    column_fold = lax.rem(lax.broadcasted_iota(jnp.int32, (columns, rows), 0), FOLDS).astype(F32)
    mask[...] = jnp.where(labels[0:1, :] != column_fold, 1.0, 0.0)
    kept[...] = mask[...] * labels[1:2, :]
    ranks = lax.broadcasted_iota(jnp.int32, (rows, width), 0)
    lane = lax.broadcasted_iota(jnp.int32, (rows, width), 1)
    for owner in range(count):
        span = slice(owner * width, (owner + 1) * width)
        later[:, span] = jnp.where(reach[owner] >= ranks, 1.0, 0.0).astype(BF16)
        earlier[:, span] = jnp.where(back[owner] >= ranks, 1.0, 0.0).astype(BF16)

    place_in[me] = place_out[me]
    block = jnp.zeros((rows, width), jnp.int32)
    def land_p(step):
        owner = peer(step + 1)
        arrive(place_out.at[owner], place_in.at[owner], p_ss, p_rs, owner)
        send(place_out.at[owner], place_in.at[me], p_ss, p_rs, owner).wait_send()
    each(count - 1, land_p)
    for owner in range(1, count):
        block += jnp.where(place_in[owner] == ranks, owner, 0)
    block = jnp.broadcast_to(jnp.sum(block, axis=1, keepdims=True), (rows, width))
    in_totals = (lane - share) == block
    for owner in range(count):
        span = slice(owner * width, (owner + 1) * width)
        hit = place_in[owner] == ranks
        to_time[:, span] = jnp.where(hit | in_totals, 1.0, 0.0).astype(BF16)
        to_id[:, span] = jnp.where(hit | ((lane == share) & (block > owner)), 1.0, 0.0).astype(BF16)
    spread = jnp.dot(labels[...].astype(BF16), to_time[...], preferred_element_type=F32)
    for owner in range(count):
        code_out[owner] = spread[:, owner * width:(owner + 1) * width]

    def push_l(step):
        owner = peer(step + 1)
        send(code_out.at[owner], code_in.at[me], l_ss, l_rs, owner).start()
    each(count - 1, push_l)
    code_in[me] = code_out[me]

    def land_l(step):
        owner = peer(step + 1)
        arrive(code_out.at[owner], code_in.at[owner], l_ss, l_rs, owner)
        send(code_out.at[owner], code_in.at[me], l_ss, l_rs, owner).wait_send()
    each(count - 1, land_l)
    labels_time = jnp.zeros((labels.shape[0], rows), F32)
    for owner in range(count):
        labels_time += across(
            code_in[owner].astype(BF16), jnp.where(spot[owner] == ranks, 1.0, 0.0).astype(BF16)
        )
    kept_time[...] = jnp.where(labels_time[0:1, :] != column_fold, 1.0, 0.0) * labels_time[1:2, :]

    def fill(step):
        low[step] = coef_in[:, piece(step)].astype(BF16)

    each(count, fill)
    shard[...] = coef_in[:, piece(me)]
    load.wait()

    def one_step(turn, carry):
        pred[...] = jnp.zeros_like(pred)

        def add_part(owner):
            pred[...] += across(low[owner], geno[:, piece(owner)])

        def add_down(step):
            owner = down(step + 1)

            @pl.when(turn > 0)
            def _():
                arrive(low.at[owner], low.at[owner], c_ss, c_rs, owner)
                relay(low.at[owner], low.at[owner], fwd_ss, c_rs, owner).start()
            add_part(owner)

        def add_side(step):
            owner = down(step) + side

            @pl.when(turn > 0)
            def _():
                arrive(low.at[owner], low.at[owner], c_ss, c_rs, owner)
            add_part(owner)

        add_part(me)
        each(half - 1, add_down)
        each(half, add_side)
        half_send[...] = pred[...]
        slot = lax.rem(turn, 2)
        swap = pltpu.make_async_remote_copy(
            src_ref=half_send, dst_ref=half_recv.at[slot], send_sem=half_ss, recv_sem=half_rs.at[slot],
            device_id={"var": 1 - var}, device_id_type=MESH,
        )
        swap.start()
        swap.wait()

        @pl.when(turn > 0)
        def _():
            def drained(step):
                owner = down(step + 1)
                send(low.at[me], low.at[me], c_ss, c_rs, owner).wait_send()
                relay(low.at[owner], low.at[owner], fwd_ss, c_rs, owner).wait_send()
            each(half - 1, drained)
            send(low.at[me], low.at[me], c_ss, c_rs, me + side).wait_send()

        weight = mask[...] * jnp.exp((half_send[...] + half_recv[slot]) * scale_vars)
        pred[...] = weight
        spread = dot2(weight, to_time[...])
        for owner in range(count):
            out_a[owner] = spread[:, owner * width:(owner + 1) * width]

        def push_a(step):
            owner = peer(step + 1)
            send(out_a.at[owner], in_a.at[me], a_ss, a_rs, owner).start()
        each(count - 1, push_a)
        risk = across2(out_a[me], later[:, slots(me)])
        for step in range(count - 1):
            owner = peer(step + 1)
            arrive(out_a.at[owner], in_a.at[owner], a_ss, a_rs, owner)
            risk += across2(in_a[owner], later[:, slots(owner)])
        events = kept_time[...]
        ratio = events / jnp.where(events > 0, risk, 1.0)
        spread = dot2(ratio, earlier[...])
        for owner in range(count):
            out_b[owner] = spread[:, owner * width:(owner + 1) * width]

        def push_b(step):
            owner = peer(step + 1)
            send(out_b.at[owner], in_b.at[me], b_ss, b_rs, owner).start()
        each(count - 1, push_b)
        hazard = across2(out_b[me], to_id[:, slots(me)])
        for step in range(count - 1):
            owner = peer(step + 1)
            arrive(out_b.at[owner], in_b.at[owner], b_ss, b_rs, owner)
            hazard += across2(in_b[owner], to_id[:, slots(owner)])
        score_out[...] = (pred[...] * hazard - kept[...]).astype(BF16)

        def push_g(step):
            owner = peer(step + 1)
            out_g[owner] = jnp.dot(
                score_out[...], geno[:, piece(owner)], preferred_element_type=F32
            ).astype(out_g.dtype)
            send(out_g.at[owner], in_g.at[me], g_ss, g_rs, owner).start()
        each(count - 1, push_g)
        total = jnp.dot(score_out[...], geno[:, piece(me)], preferred_element_type=F32)
        for step in range(count - 1):
            owner = peer(count - 1 - step)
            arrive(out_g.at[owner], in_g.at[owner], g_ss, g_rs, owner)
            total += in_g[owner].astype(F32)
        pace = step_size[...]
        stepped = shard[...] - pace * (total * scale_samples)
        shrunk = jnp.maximum(jnp.abs(stepped) - pace * penalty[...], 0.0)
        fresh = jnp.where(stepped > 0, shrunk, -shrunk)
        shard[...] = fresh

        def drained_all(step):
            owner = peer(step + 1)
            send(out_a.at[owner], in_a.at[me], a_ss, a_rs, owner).wait_send()
            send(out_b.at[owner], in_b.at[me], b_ss, b_rs, owner).wait_send()
            send(out_g.at[owner], in_g.at[me], g_ss, g_rs, owner).wait_send()

        @pl.when(turn < ITERS - 1)
        def _():
            low[me] = fresh.astype(BF16)

            def push_c(step):
                owner = down(step + 1)
                send(low.at[me], low.at[me], c_ss, c_rs, owner).start()
            each(half - 1, push_c)
            send(low.at[me], low.at[me], c_ss, c_rs, me + side).start()

        each(count - 1, drained_all)
        return carry

    lax.fori_loop(0, ITERS, one_step, 0)

    coef_out[:, piece(me)] = shard[...]

    def push_f(step):
        owner = down(step + 1)
        send(shard, coef_out.at[:, piece(me)], f_ss, f_rs, owner).start()
    each(half - 1, push_f)
    send(shard, coef_out.at[:, piece(me)], f_ss, f_rs, me + side).start()

    def pass_f(step):
        owner = down(step + 1)
        arrive(shard, coef_out.at[:, piece(owner)], f_ss, f_rs, owner)
        relay(coef_out.at[:, piece(owner)], coef_out.at[:, piece(owner)], last_ss, f_rs, owner).start()
    each(half - 1, pass_f)

    def land_f(step):
        owner = down(step) + side
        arrive(shard, coef_out.at[:, piece(owner)], f_ss, f_rs, owner)
    each(half, land_f)

    def done_f(step):
        owner = down(step + 1)
        send(shard, coef_out.at[:, piece(me)], f_ss, f_rs, owner).wait_send()
        relay(coef_out.at[:, piece(owner)], coef_out.at[:, piece(owner)], last_ss, f_rs, owner).wait_send()
    each(half - 1, done_f)
    send(shard, coef_out.at[:, piece(me)], f_ss, f_rs, me + side).wait_send()


def local(genotypes, coefficients, time_order, fold_label, event_flag, penalty, step_size):
    rows = genotypes.shape[0]
    columns, variants = coefficients.shape
    count = lax.axis_size("samp")
    me = lax.axis_index("samp")
    share = rows // count
    width = -(-(share + count) // 128) * 128
    total = count * width
    part = variants // count

    ranks = jnp.arange(rows, dtype=jnp.int32)
    slot_all = jnp.arange(total, dtype=jnp.int32)
    lane = slot_all % width
    owner = time_order // rows
    place = time_order % rows
    same = (owner[:, None] == owner[None, :]) & (ranks[:, None] < ranks[None, :])
    key = owner * width + jnp.sum(same.astype(jnp.int32), axis=0)
    match = key[:, None] == slot_all[None, :]
    rank_of = jnp.max(jnp.where(match, ranks[:, None], -1), axis=0)
    place_of = jnp.max(jnp.where(match, place[:, None], -1), axis=0)
    in_totals = (lane >= share) & (lane < share + count)
    spot = jnp.where(lane < share, rank_of, -1)
    reach = jnp.where(in_totals & (lane - share > me), rows, spot)
    back = jnp.where(lane == share, rows, spot)
    labels = jnp.stack([fold_label, event_flag]).astype(F32)
    labels = jnp.concatenate([labels, jnp.zeros((6, rows), F32)])
    place_of, reach, back, spot = (value.reshape(count, 1, width) for value in (place_of, reach, back, spot))

    vmem = pl.BlockSpec(memory_space=pltpu.VMEM)
    dma = pltpu.SemaphoreType.DMA
    return pl.pallas_call(
        functools.partial(path_kernel, count, 1.0 / math.sqrt(VARS), 1.0 / math.sqrt(rows * count)),
        out_shape=(
            jax.ShapeDtypeStruct((columns, variants), F32),
            jax.ShapeDtypeStruct((columns, rows), BF16),
        ),
        in_specs=[pl.BlockSpec(memory_space=pl.ANY)] + [vmem] * 8,
        out_specs=(vmem, vmem),
        scratch_shapes=[
            pltpu.VMEM((rows, variants), BF16),
            pltpu.VMEM((rows, total), BF16),
            pltpu.VMEM((rows, total), BF16),
            pltpu.VMEM((rows, total), BF16),
            pltpu.VMEM((rows, total), BF16),
            pltpu.VMEM((columns, rows), F32),
            pltpu.VMEM((columns, rows), F32),
            pltpu.VMEM((columns, rows), F32),
            pltpu.VMEM((count, 1, width), jnp.int32),
            pltpu.VMEM((count, 8, width), F32),
            pltpu.VMEM((count, 8, width), F32),
            pltpu.VMEM((count, columns, part), BF16),
            pltpu.VMEM((columns, part), F32),
            pltpu.VMEM((columns, rows), F32),
            pltpu.VMEM((2, columns, rows), F32),
            pltpu.VMEM((count, columns, width), F32),
            pltpu.VMEM((count, columns, width), F32),
            pltpu.VMEM((count, columns, width), F32),
            pltpu.VMEM((count, columns, width), F32),
            pltpu.VMEM((count, columns, part), BF16),
            pltpu.VMEM((count, columns, part), BF16),
            pltpu.VMEM((columns, rows), F32),
            dma,
        ] + [dma((count,))] * 6 + [
            dma, dma((2,)),
        ] + [dma((count,))] * 10,
        compiler_params=pltpu.CompilerParams(
            collective_id=0, has_side_effects=True, vmem_limit_bytes=60 * 1024 * 1024
        ),
    )(
        genotypes, coefficients, labels, place_of, reach, back, spot,
        step_size[:, None], penalty[:, None],
    )


def solution(mesh):
    placed = (
        P("samp", "var"),
        P("pheno", "var"),
        P(("pheno", "samp")),
        P(("pheno", "samp")),
        P(("pheno", "samp")),
        P(),
        P(),
    )
    return jax.shard_map(
        local,
        mesh=mesh,
        in_specs=placed,
        out_specs=(P("pheno", "var"), P("pheno", "samp")),
        check_vma=False,
    )
```

```python
import functools
import math

import jax
import jax.numpy as jnp
from jax import lax
from jax.experimental import pallas as pl
from jax.experimental.pallas import tpu as pltpu
from jax.sharding import PartitionSpec as P

VARS = 16384
FOLDS = 8
ITERS = 3
MESH = pl.DeviceIdType.MESH
CUTS = 4
F32 = jnp.float32
BF16 = jnp.bfloat16


def each(count, body):
    if count <= 8:
        for step in range(count):
            body(step)
    else:
        lax.fori_loop(0, count, lambda step, carry: (body(step), carry)[1], 0)


def halves(value):
    high = value.astype(BF16)
    low = (value - high.astype(F32)).astype(BF16)
    return jnp.concatenate([high, low], axis=0)


def across(left, right):
    return lax.dot_general(left, right, (((1,), (1,)), ((), ())), preferred_element_type=F32)


def across2(value, matrix):
    rows = value.shape[0]
    both = across(halves(value), matrix)
    return both[:rows] + both[rows:]


def dot2(value, matrix):
    rows = value.shape[0]
    both = jnp.dot(halves(value), matrix, preferred_element_type=F32)
    return both[:rows] + both[rows:]


def path_kernel(
    count, scale_vars, scale_samples,
    geno_in, coef_in, fold_row, event_row, place_out, reach, back, spot, step_row, penalty_row,
    coef_out, score_out,
    geno, to_time, later, earlier, to_id, mask, kept, kept_time, place_in, code_out, code_in,
    low, shard, half_send, half_recv, out_a, in_a, out_b, in_b, out_g, in_g, pred,
    load_sem, p_ss, p_rs, l_ss, l_rs, fwd_ss, last_ss, half_ss, half_rs, a_ss, a_rs, b_ss, b_rs, g_ss, g_rs, c_ss, c_rs, f_ss, f_rs,
):
    me = lax.axis_index("samp")
    var = lax.axis_index("var")
    columns, variants = coef_in.shape
    rows = geno.shape[0]
    part = variants // count
    width = later.shape[1] // count
    share = rows // count
    half = count // 2
    load = pltpu.make_async_copy(geno_in, geno, load_sem)
    load.start()

    def peer(step):
        return lax.rem(me + step, count)

    def piece(owner):
        return pl.ds(pl.multiple_of(owner * part, part), part)

    side = 1 - 2 * lax.rem(me, 2)

    def down(step):
        return lax.rem(me + 2 * step, count)

    cuts = min(CUTS, part // 128)
    cut = part // cuts

    def bit(owner, number):
        return low.at[owner, :, pl.ds(number * cut, cut)]

    def wide(owner, number):
        return coef_out.at[:, pl.ds(pl.multiple_of(owner * part + number * cut, cut), cut)]

    def send_to(spot_of, ssem, rsem, number, owner):
        return pltpu.make_async_remote_copy(
            src_ref=spot_of(me, number), dst_ref=spot_of(me, number),
            send_sem=ssem.at[owner, number], recv_sem=rsem.at[me, number],
            device_id={"samp": owner}, device_id_type=MESH,
        )

    def pass_on(spot_of, ssem, rsem, number, owner):
        return pltpu.make_async_remote_copy(
            src_ref=spot_of(owner, number), dst_ref=spot_of(owner, number),
            send_sem=ssem.at[owner, number], recv_sem=rsem.at[owner, number],
            device_id={"samp": me + side}, device_id_type=MESH,
        )

    def spread_out(spot_of, ssem, rsem):
        for number in range(cuts):
            def go(step):
                send_to(spot_of, ssem, rsem, number, down(step + 1)).start()
            send_to(spot_of, ssem, rsem, number, me + side).start()
            each(half - 1, go)

    def relay_all(spot_of, ssem, rsem):
        for number in range(cuts):
            def go(step):
                copy = pass_on(spot_of, ssem, rsem, number, down(step + 1))
                copy.wait_recv()
                copy.start()
            each(half - 1, go)

    def land(spot_of, ssem, rsem, owner):
        for number in range(cuts):
            pass_on(spot_of, ssem, rsem, number, owner).wait_recv()

    def settle(spot_of, ssem, fsem, rsem):
        for number in range(cuts):
            def go(step):
                owner = down(step + 1)
                send_to(spot_of, ssem, rsem, number, owner).wait_send()
                pass_on(spot_of, fsem, rsem, number, owner).wait_send()
            each(half - 1, go)
            send_to(spot_of, ssem, rsem, number, me + side).wait_send()

    def slots(owner):
        return pl.ds(pl.multiple_of(owner * width, width), width)

    barrier = pltpu.get_barrier_semaphore()

    def greet(step):
        pl.semaphore_signal(barrier, inc=1, device_id={"samp": peer(step + 1)}, device_id_type=MESH)

    each(count - 1, greet)
    pl.semaphore_signal(barrier, inc=1, device_id={"var": 1 - var}, device_id_type=MESH)
    pl.semaphore_wait(barrier, count)

    def send(source, target, ssem, rsem, owner):
        return pltpu.make_async_remote_copy(
            src_ref=source,
            dst_ref=target,
            send_sem=ssem.at[owner],
            recv_sem=rsem.at[me],
            device_id={"samp": owner},
            device_id_type=MESH,
        )

    def arrive(source, target, ssem, rsem, owner):
        pltpu.make_async_remote_copy(
            src_ref=source,
            dst_ref=target,
            send_sem=ssem.at[owner],
            recv_sem=rsem.at[owner],
            device_id={"samp": owner},
            device_id_type=MESH,
        ).wait_recv()

    def push_p(step):
        owner = peer(step + 1)
        send(place_out.at[owner], place_in.at[me], p_ss, p_rs, owner).start()
    each(count - 1, push_p)

    line = lax.broadcasted_iota(jnp.int32, (8, rows), 0)
    labels = jnp.where(line == 0, fold_row[...], jnp.where(line == 1, event_row[...], 0)).astype(F32)
    same = lax.broadcasted_iota(jnp.int32, (columns, columns), 0) == lax.broadcasted_iota(
        jnp.int32, (columns, columns), 1
    )
    pace = jnp.sum(jnp.where(same, step_row[...], 0.0), axis=1, keepdims=True)
    threshold = pace * jnp.sum(jnp.where(same, penalty_row[...], 0.0), axis=1, keepdims=True)
    column_fold = lax.rem(lax.broadcasted_iota(jnp.int32, (columns, rows), 0), FOLDS).astype(F32)
    mask[...] = jnp.where(labels[0:1, :] != column_fold, 1.0, 0.0)
    kept[...] = mask[...] * labels[1:2, :]
    ranks = lax.broadcasted_iota(jnp.int32, (rows, width), 0)
    lane = lax.broadcasted_iota(jnp.int32, (rows, width), 1)
    for owner in range(count):
        span = slice(owner * width, (owner + 1) * width)
        later[:, span] = jnp.where(reach[owner] >= ranks, 1.0, 0.0).astype(BF16)
        earlier[:, span] = jnp.where(back[owner] >= ranks, 1.0, 0.0).astype(BF16)

    place_in[me] = place_out[me]
    block = jnp.zeros((rows, width), jnp.int32)
    def land_p(step):
        owner = peer(step + 1)
        arrive(place_out.at[owner], place_in.at[owner], p_ss, p_rs, owner)
        send(place_out.at[owner], place_in.at[me], p_ss, p_rs, owner).wait_send()
    each(count - 1, land_p)
    for owner in range(1, count):
        block += jnp.where(place_in[owner] == ranks, owner, 0)
    block = jnp.broadcast_to(jnp.sum(block, axis=1, keepdims=True), (rows, width))
    in_totals = (lane - share) == block
    for owner in range(count):
        span = slice(owner * width, (owner + 1) * width)
        hit = place_in[owner] == ranks
        to_time[:, span] = jnp.where(hit | in_totals, 1.0, 0.0).astype(BF16)
        to_id[:, span] = jnp.where(hit | ((lane == share) & (block > owner)), 1.0, 0.0).astype(BF16)
    spread = jnp.dot(labels.astype(BF16), to_time[...], preferred_element_type=F32)
    for owner in range(count):
        code_out[owner] = spread[:, owner * width:(owner + 1) * width]

    def push_l(step):
        owner = peer(step + 1)
        send(code_out.at[owner], code_in.at[me], l_ss, l_rs, owner).start()
    each(count - 1, push_l)
    code_in[me] = code_out[me]

    def land_l(step):
        owner = peer(step + 1)
        arrive(code_out.at[owner], code_in.at[owner], l_ss, l_rs, owner)
        send(code_out.at[owner], code_in.at[me], l_ss, l_rs, owner).wait_send()
    each(count - 1, land_l)
    labels_time = jnp.zeros((labels.shape[0], rows), F32)
    for owner in range(count):
        labels_time += across(
            code_in[owner].astype(BF16), jnp.where(spot[owner] == ranks, 1.0, 0.0).astype(BF16)
        )
    kept_time[...] = jnp.where(labels_time[0:1, :] != column_fold, 1.0, 0.0) * labels_time[1:2, :]

    def fill(step):
        low[step] = coef_in[:, piece(step)].astype(BF16)

    each(count, fill)
    shard[...] = coef_in[:, piece(me)]
    load.wait()

    def one_step(turn, carry):
        pred[...] = jnp.zeros_like(pred)

        def add_part(owner):
            pred[...] += across(low[owner], geno[:, piece(owner)])

        def add_down(step):
            add_part(down(step + 1))

        def add_side(step):
            owner = down(step) + side

            @pl.when(turn > 0)
            def _():
                land(bit, c_ss, c_rs, owner)
            add_part(owner)

        add_part(me)

        @pl.when(turn > 0)
        def _():
            relay_all(bit, fwd_ss, c_rs)
        each(half - 1, add_down)
        each(half, add_side)
        half_send[...] = pred[...]
        slot = lax.rem(turn, 2)
        swap = pltpu.make_async_remote_copy(
            src_ref=half_send, dst_ref=half_recv.at[slot], send_sem=half_ss, recv_sem=half_rs.at[slot],
            device_id={"var": 1 - var}, device_id_type=MESH,
        )
        swap.start()
        swap.wait()

        @pl.when(turn > 0)
        def _():
            settle(bit, c_ss, fwd_ss, c_rs)

        weight = mask[...] * jnp.exp((half_send[...] + half_recv[slot]) * scale_vars)
        pred[...] = weight
        spread = dot2(weight, to_time[...])
        for owner in range(count):
            out_a[owner] = spread[:, owner * width:(owner + 1) * width]

        def push_a(step):
            owner = peer(step + 1)
            send(out_a.at[owner], in_a.at[me], a_ss, a_rs, owner).start()
        each(count - 1, push_a)
        risk = across2(out_a[me], later[:, slots(me)])
        for step in range(count - 1):
            owner = peer(step + 1)
            arrive(out_a.at[owner], in_a.at[owner], a_ss, a_rs, owner)
            risk += across2(in_a[owner], later[:, slots(owner)])
        events = kept_time[...]
        ratio = events / jnp.where(events > 0, risk, 1.0)
        spread = dot2(ratio, earlier[...])
        for owner in range(count):
            out_b[owner] = spread[:, owner * width:(owner + 1) * width]

        def push_b(step):
            owner = peer(step + 1)
            send(out_b.at[owner], in_b.at[me], b_ss, b_rs, owner).start()
        each(count - 1, push_b)
        hazard = across2(out_b[me], to_id[:, slots(me)])
        for step in range(count - 1):
            owner = peer(step + 1)
            arrive(out_b.at[owner], in_b.at[owner], b_ss, b_rs, owner)
            hazard += across2(in_b[owner], to_id[:, slots(owner)])
        score_out[...] = (pred[...] * hazard - kept[...]).astype(BF16)

        def push_g(step):
            owner = peer(step + 1)
            out_g[owner] = jnp.dot(
                score_out[...], geno[:, piece(owner)], preferred_element_type=F32
            ).astype(out_g.dtype)
            send(out_g.at[owner], in_g.at[me], g_ss, g_rs, owner).start()
        each(count - 1, push_g)
        total = jnp.dot(score_out[...], geno[:, piece(me)], preferred_element_type=F32)
        for step in range(count - 1):
            owner = peer(count - 1 - step)
            arrive(out_g.at[owner], in_g.at[owner], g_ss, g_rs, owner)
            total += in_g[owner].astype(F32)
        stepped = shard[...] - pace * (total * scale_samples)
        shrunk = jnp.maximum(jnp.abs(stepped) - threshold, 0.0)
        fresh = jnp.where(stepped > 0, shrunk, -shrunk)
        shard[...] = fresh

        def drained_all(step):
            owner = peer(step + 1)
            send(out_a.at[owner], in_a.at[me], a_ss, a_rs, owner).wait_send()
            send(out_b.at[owner], in_b.at[me], b_ss, b_rs, owner).wait_send()
            send(out_g.at[owner], in_g.at[me], g_ss, g_rs, owner).wait_send()

        @pl.when(turn < ITERS - 1)
        def _():
            low[me] = fresh.astype(BF16)

            spread_out(bit, c_ss, c_rs)

        each(count - 1, drained_all)
        return carry

    lax.fori_loop(0, ITERS, one_step, 0)

    coef_out[:, piece(me)] = shard[...]

    spread_out(wide, f_ss, f_rs)
    relay_all(wide, last_ss, f_rs)

    def land_f(step):
        land(wide, f_ss, f_rs, down(step) + side)
    each(half, land_f)
    settle(wide, f_ss, last_ss, f_rs)


def local(genotypes, coefficients, time_order, fold_label, event_flag, penalty, step_size):
    rows = genotypes.shape[0]
    columns, variants = coefficients.shape
    count = lax.axis_size("samp")
    me = lax.axis_index("samp")
    share = rows // count
    width = -(-(share + count) // 128) * 128
    total = count * width
    part = variants // count

    ranks = jnp.arange(rows, dtype=jnp.int32)
    slot_all = jnp.arange(total, dtype=jnp.int32)
    lane = slot_all % width
    owner = time_order // rows
    place = time_order % rows
    same = (owner[:, None] == owner[None, :]) & (ranks[:, None] < ranks[None, :])
    key = owner * width + jnp.sum(same.astype(jnp.int32), axis=0)
    match = key[:, None] == slot_all[None, :]
    rank_of = jnp.max(jnp.where(match, ranks[:, None], -1), axis=0)
    place_of = jnp.max(jnp.where(match, place[:, None], -1), axis=0)
    in_totals = (lane >= share) & (lane < share + count)
    spot = jnp.where(lane < share, rank_of, -1)
    reach = jnp.where(in_totals & (lane - share > me), rows, spot)
    back = jnp.where(lane == share, rows, spot)
    place_of, reach, back, spot = (value.reshape(count, 1, width) for value in (place_of, reach, back, spot))

    vmem = pl.BlockSpec(memory_space=pltpu.VMEM)
    dma = pltpu.SemaphoreType.DMA
    return pl.pallas_call(
        functools.partial(path_kernel, count, 1.0 / math.sqrt(VARS), 1.0 / math.sqrt(rows * count)),
        out_shape=(
            jax.ShapeDtypeStruct((columns, variants), F32),
            jax.ShapeDtypeStruct((columns, rows), BF16),
        ),
        in_specs=[pl.BlockSpec(memory_space=pl.ANY)] + [vmem] * 9,
        out_specs=(vmem, vmem),
        scratch_shapes=[
            pltpu.VMEM((rows, variants), BF16),
            pltpu.VMEM((rows, total), BF16),
            pltpu.VMEM((rows, total), BF16),
            pltpu.VMEM((rows, total), BF16),
            pltpu.VMEM((rows, total), BF16),
            pltpu.VMEM((columns, rows), F32),
            pltpu.VMEM((columns, rows), F32),
            pltpu.VMEM((columns, rows), F32),
            pltpu.VMEM((count, 1, width), jnp.int32),
            pltpu.VMEM((count, 8, width), F32),
            pltpu.VMEM((count, 8, width), F32),
            pltpu.VMEM((count, columns, part), BF16),
            pltpu.VMEM((columns, part), F32),
            pltpu.VMEM((columns, rows), F32),
            pltpu.VMEM((2, columns, rows), F32),
            pltpu.VMEM((count, columns, width), F32),
            pltpu.VMEM((count, columns, width), F32),
            pltpu.VMEM((count, columns, width), F32),
            pltpu.VMEM((count, columns, width), F32),
            pltpu.VMEM((count, columns, part), BF16),
            pltpu.VMEM((count, columns, part), BF16),
            pltpu.VMEM((columns, rows), F32),
            dma,
        ] + [dma((count,))] * 4 + [dma((count, CUTS))] * 2 + [
            dma, dma((2,)),
        ] + [dma((count,))] * 6 + [dma((count, CUTS))] * 4,
        compiler_params=pltpu.CompilerParams(
            collective_id=0, has_side_effects=True, vmem_limit_bytes=60 * 1024 * 1024
        ),
    )(
        genotypes, coefficients, fold_label[None], event_flag[None], place_of, reach, back, spot,
        step_size[None], penalty[None],
    )


def solution(mesh):
    placed = (
        P("samp", "var"),
        P("pheno", "var"),
        P(("pheno", "samp")),
        P(("pheno", "samp")),
        P(("pheno", "samp")),
        P(),
        P(),
    )
    return jax.shard_map(
        local,
        mesh=mesh,
        in_specs=placed,
        out_specs=(P("pheno", "var"), P("pheno", "samp")),
        check_vma=False,
    )
```

```python
import functools
import math

import jax
import jax.numpy as jnp
from jax import lax
from jax.experimental import pallas as pl
from jax.experimental.pallas import tpu as pltpu
from jax.sharding import PartitionSpec as P

VARS = 16384
FOLDS = 8
ITERS = 3
MESH = pl.DeviceIdType.MESH
CUTS = 8
F32 = jnp.float32
BF16 = jnp.bfloat16


def each(count, body):
    if count <= 8:
        for step in range(count):
            body(step)
    else:
        lax.fori_loop(0, count, lambda step, carry: (body(step), carry)[1], 0)


def halves(value):
    high = value.astype(BF16)
    low = (value - high.astype(F32)).astype(BF16)
    return jnp.concatenate([high, low], axis=0)


def across(left, right):
    return lax.dot_general(left, right, (((1,), (1,)), ((), ())), preferred_element_type=F32)


def across2(value, matrix):
    rows = value.shape[0]
    both = across(halves(value), matrix)
    return both[:rows] + both[rows:]


def dot2(value, matrix):
    rows = value.shape[0]
    both = jnp.dot(halves(value), matrix, preferred_element_type=F32)
    return both[:rows] + both[rows:]


def path_kernel(
    count, scale_vars, scale_samples,
    geno_in, coef_in, code_row, place_out, reach, back, spot, step_row, penalty_row,
    coef_out, score_out,
    geno, to_time, later, earlier, to_id, mask, kept, kept_time, place_in, code_out, code_in,
    low, shard, half_send, half_recv, out_a, in_a, out_b, in_b, out_g, in_g, pred, held, s_ss, s_rs,
    load_sem, p_ss, p_rs, l_ss, l_rs, fwd_ss, last_ss, half_ss, half_rs, a_ss, a_rs, b_ss, b_rs, g_ss, g_rs, c_ss, c_rs, f_ss, f_rs,
):
    me = lax.axis_index("samp")
    var = lax.axis_index("var")
    columns, variants = coef_in.shape
    rows = geno.shape[0]
    part = variants // count
    width = later.shape[1] // count
    share = rows // count
    half = count // 2
    few = columns // 2
    mine = pl.ds(pl.multiple_of(var * few, few), few)
    theirs = pl.ds(pl.multiple_of((1 - var) * few, few), few)
    load = pltpu.make_async_copy(geno_in, geno, load_sem)
    load.start()

    def peer(step):
        return lax.rem(me + step, count)

    def piece(owner):
        return pl.ds(pl.multiple_of(owner * part, part), part)

    side = 1 - 2 * lax.rem(me, 2)

    def down(step):
        return lax.rem(me + 2 * step, count)

    cuts = min(CUTS, part // 128)
    cut = part // cuts

    def bit(owner, number):
        return low.at[owner, :, pl.ds(number * cut, cut)]

    def wide(owner, number):
        return coef_out.at[:, pl.ds(pl.multiple_of(owner * part + number * cut, cut), cut)]

    def send_to(spot_of, ssem, rsem, number, owner):
        return pltpu.make_async_remote_copy(
            src_ref=spot_of(me, number), dst_ref=spot_of(me, number),
            send_sem=ssem.at[owner, number], recv_sem=rsem.at[me, number],
            device_id={"samp": owner}, device_id_type=MESH,
        )

    def pass_on(spot_of, ssem, rsem, number, owner):
        return pltpu.make_async_remote_copy(
            src_ref=spot_of(owner, number), dst_ref=spot_of(owner, number),
            send_sem=ssem.at[owner, number], recv_sem=rsem.at[owner, number],
            device_id={"samp": me + side}, device_id_type=MESH,
        )

    def spread_out(spot_of, ssem, rsem):
        for number in range(cuts):
            def go(step):
                send_to(spot_of, ssem, rsem, number, down(step + 1)).start()
            send_to(spot_of, ssem, rsem, number, me + side).start()
            each(half - 1, go)

    def relay_all(spot_of, ssem, rsem):
        for number in range(cuts):
            def go(step):
                copy = pass_on(spot_of, ssem, rsem, number, down(step + 1))
                copy.wait_recv()
                copy.start()
            each(half - 1, go)

    def land(spot_of, ssem, rsem, owner):
        for number in range(cuts):
            pass_on(spot_of, ssem, rsem, number, owner).wait_recv()

    def settle(spot_of, ssem, fsem, rsem):
        for number in range(cuts):
            def go(step):
                owner = down(step + 1)
                send_to(spot_of, ssem, rsem, number, owner).wait_send()
                pass_on(spot_of, fsem, rsem, number, owner).wait_send()
            each(half - 1, go)
            send_to(spot_of, ssem, rsem, number, me + side).wait_send()

    def slots(owner):
        return pl.ds(pl.multiple_of(owner * width, width), width)

    barrier = pltpu.get_barrier_semaphore()

    def greet(step):
        pl.semaphore_signal(barrier, inc=1, device_id={"samp": peer(step + 1)}, device_id_type=MESH)

    each(count - 1, greet)
    pl.semaphore_signal(barrier, inc=1, device_id={"var": 1 - var}, device_id_type=MESH)
    pl.semaphore_wait(barrier, count)

    def send(source, target, ssem, rsem, owner):
        return pltpu.make_async_remote_copy(
            src_ref=source,
            dst_ref=target,
            send_sem=ssem.at[owner],
            recv_sem=rsem.at[me],
            device_id={"samp": owner},
            device_id_type=MESH,
        )

    def arrive(source, target, ssem, rsem, owner):
        pltpu.make_async_remote_copy(
            src_ref=source,
            dst_ref=target,
            send_sem=ssem.at[owner],
            recv_sem=rsem.at[owner],
            device_id={"samp": owner},
            device_id_type=MESH,
        ).wait_recv()

    def push_p(step):
        owner = peer(step + 1)
        send(place_out.at[owner], place_in.at[me], p_ss, p_rs, owner).start()
    each(count - 1, push_p)

    line = lax.broadcasted_iota(jnp.int32, (8, rows), 0)
    labels = jnp.where(line == 0, code_row[...] // 2, jnp.where(line == 1, code_row[...] % 2, 0)).astype(F32)
    same = lax.broadcasted_iota(jnp.int32, (columns, columns), 0) == lax.broadcasted_iota(
        jnp.int32, (columns, columns), 1
    )
    pace = jnp.sum(jnp.where(same, step_row[...], 0.0), axis=1, keepdims=True)
    threshold = pace * jnp.sum(jnp.where(same, penalty_row[...], 0.0), axis=1, keepdims=True)
    column_fold = lax.rem(lax.broadcasted_iota(jnp.int32, (few, rows), 0) + var * few, FOLDS).astype(F32)
    mask[...] = jnp.where(labels[0:1, :] != column_fold, 1.0, 0.0)
    kept[...] = mask[...] * labels[1:2, :]
    ranks = lax.broadcasted_iota(jnp.int32, (rows, width), 0)
    lane = lax.broadcasted_iota(jnp.int32, (rows, width), 1)
    for owner in range(count):
        span = slice(owner * width, (owner + 1) * width)
        later[:, span] = jnp.where(reach[owner] >= ranks, 1.0, 0.0).astype(BF16)
        earlier[:, span] = jnp.where(back[owner] >= ranks, 1.0, 0.0).astype(BF16)

    place_in[me] = place_out[me]
    block = jnp.zeros((rows, width), jnp.int32)
    def land_p(step):
        owner = peer(step + 1)
        arrive(place_out.at[owner], place_in.at[owner], p_ss, p_rs, owner)
        send(place_out.at[owner], place_in.at[me], p_ss, p_rs, owner).wait_send()
    each(count - 1, land_p)
    for owner in range(1, count):
        block += jnp.where(place_in[owner] == ranks, owner, 0)
    block = jnp.broadcast_to(jnp.sum(block, axis=1, keepdims=True), (rows, width))
    in_totals = (lane - share) == block
    for owner in range(count):
        span = slice(owner * width, (owner + 1) * width)
        hit = place_in[owner] == ranks
        to_time[:, span] = jnp.where(hit | in_totals, 1.0, 0.0).astype(BF16)
        to_id[:, span] = jnp.where(hit | ((lane == share) & (block > owner)), 1.0, 0.0).astype(BF16)
    spread = jnp.dot(labels.astype(BF16), to_time[...], preferred_element_type=F32)
    for owner in range(count):
        code_out[owner] = spread[:, owner * width:(owner + 1) * width]

    def push_l(step):
        owner = peer(step + 1)
        send(code_out.at[owner], code_in.at[me], l_ss, l_rs, owner).start()
    each(count - 1, push_l)
    code_in[me] = code_out[me]

    def land_l(step):
        owner = peer(step + 1)
        arrive(code_out.at[owner], code_in.at[owner], l_ss, l_rs, owner)
        send(code_out.at[owner], code_in.at[me], l_ss, l_rs, owner).wait_send()
    each(count - 1, land_l)
    labels_time = jnp.zeros((labels.shape[0], rows), F32)
    for owner in range(count):
        labels_time += across(
            code_in[owner].astype(BF16), jnp.where(spot[owner] == ranks, 1.0, 0.0).astype(BF16)
        )
    kept_time[...] = jnp.where(labels_time[0:1, :] != column_fold, 1.0, 0.0) * labels_time[1:2, :]

    def fill(step):
        low[step] = coef_in[:, piece(step)].astype(BF16)

    each(count, fill)
    shard[...] = coef_in[:, piece(me)]
    load.wait()

    def one_step(turn, carry):
        pred[...] = jnp.zeros_like(pred)

        def add_part(owner):
            pred[...] += across(low[owner], geno[:, piece(owner)])

        def add_down(step):
            add_part(down(step + 1))

        def add_side(step):
            owner = down(step) + side

            @pl.when(turn > 0)
            def _():
                land(bit, c_ss, c_rs, owner)
            add_part(owner)

        add_part(me)

        @pl.when(turn > 0)
        def _():
            relay_all(bit, fwd_ss, c_rs)
        each(half - 1, add_down)
        each(half, add_side)
        half_send[...] = pred[theirs, :]
        slot = lax.rem(turn, 2)
        swap = pltpu.make_async_remote_copy(
            src_ref=half_send, dst_ref=half_recv.at[slot], send_sem=half_ss, recv_sem=half_rs.at[slot],
            device_id={"var": 1 - var}, device_id_type=MESH,
        )
        swap.start()
        swap.wait()

        @pl.when(turn > 0)
        def _():
            settle(bit, c_ss, fwd_ss, c_rs)

        weight = mask[...] * jnp.exp((pred[mine, :] + half_recv[slot]) * scale_vars)
        held[...] = weight
        spread = dot2(weight, to_time[...])
        for owner in range(count):
            out_a[owner] = spread[:, owner * width:(owner + 1) * width]

        def push_a(step):
            owner = peer(step + 1)
            send(out_a.at[owner], in_a.at[me], a_ss, a_rs, owner).start()
        each(count - 1, push_a)
        risk = across2(out_a[me], later[:, slots(me)])
        for step in range(count - 1):
            owner = peer(step + 1)
            arrive(out_a.at[owner], in_a.at[owner], a_ss, a_rs, owner)
            risk += across2(in_a[owner], later[:, slots(owner)])
        events = kept_time[...]
        ratio = events / jnp.where(events > 0, risk, 1.0)
        spread = dot2(ratio, earlier[...])
        for owner in range(count):
            out_b[owner] = spread[:, owner * width:(owner + 1) * width]

        def push_b(step):
            owner = peer(step + 1)
            send(out_b.at[owner], in_b.at[me], b_ss, b_rs, owner).start()
        each(count - 1, push_b)
        hazard = across2(out_b[me], to_id[:, slots(me)])
        for step in range(count - 1):
            owner = peer(step + 1)
            arrive(out_b.at[owner], in_b.at[owner], b_ss, b_rs, owner)
            hazard += across2(in_b[owner], to_id[:, slots(owner)])
        score_out[mine, :] = (held[...] * hazard - kept[...]).astype(BF16)
        trade = pltpu.make_async_remote_copy(
            src_ref=score_out.at[mine, :], dst_ref=score_out.at[mine, :], send_sem=s_ss, recv_sem=s_rs,
            device_id={"var": 1 - var}, device_id_type=MESH,
        )
        trade.start()
        trade.wait()

        def push_g(step):
            owner = peer(step + 1)
            out_g[owner] = jnp.dot(
                score_out[...], geno[:, piece(owner)], preferred_element_type=F32
            ).astype(out_g.dtype)
            send(out_g.at[owner], in_g.at[me], g_ss, g_rs, owner).start()
        each(count - 1, push_g)
        total = jnp.dot(score_out[...], geno[:, piece(me)], preferred_element_type=F32)
        for step in range(count - 1):
            owner = peer(count - 1 - step)
            arrive(out_g.at[owner], in_g.at[owner], g_ss, g_rs, owner)
            total += in_g[owner].astype(F32)
        stepped = shard[...] - pace * (total * scale_samples)
        shrunk = jnp.maximum(jnp.abs(stepped) - threshold, 0.0)
        fresh = jnp.where(stepped > 0, shrunk, -shrunk)
        shard[...] = fresh

        def drained_all(step):
            owner = peer(step + 1)
            send(out_a.at[owner], in_a.at[me], a_ss, a_rs, owner).wait_send()
            send(out_b.at[owner], in_b.at[me], b_ss, b_rs, owner).wait_send()
            send(out_g.at[owner], in_g.at[me], g_ss, g_rs, owner).wait_send()

        @pl.when(turn < ITERS - 1)
        def _():
            low[me] = fresh.astype(BF16)

            spread_out(bit, c_ss, c_rs)

        each(count - 1, drained_all)
        return carry

    lax.fori_loop(0, ITERS, one_step, 0)

    coef_out[:, piece(me)] = shard[...]

    spread_out(wide, f_ss, f_rs)
    relay_all(wide, last_ss, f_rs)

    def land_f(step):
        land(wide, f_ss, f_rs, down(step) + side)
    each(half, land_f)
    settle(wide, f_ss, last_ss, f_rs)


def local(genotypes, coefficients, time_order, fold_label, event_flag, penalty, step_size):
    rows = genotypes.shape[0]
    columns, variants = coefficients.shape
    count = lax.axis_size("samp")
    me = lax.axis_index("samp")
    share = rows // count
    width = -(-(share + count) // 128) * 128
    total = count * width
    part = variants // count

    ranks = jnp.arange(rows, dtype=jnp.int32)
    slot_all = jnp.arange(total, dtype=jnp.int32)
    lane = slot_all % width
    owner = time_order // rows
    place = time_order % rows
    same = (owner[:, None] == owner[None, :]) & (ranks[:, None] < ranks[None, :])
    key = owner * width + jnp.sum(same.astype(jnp.int32), axis=0)
    match = key[:, None] == slot_all[None, :]
    rank_of = jnp.max(jnp.where(match, ranks[:, None], -1), axis=0)
    place_of = jnp.max(jnp.where(match, place[:, None], -1), axis=0)
    in_totals = (lane >= share) & (lane < share + count)
    spot = jnp.where(lane < share, rank_of, -1)
    reach = jnp.where(in_totals & (lane - share > me), rows, spot)
    back = jnp.where(lane == share, rows, spot)
    place_of, reach, back, spot = (value.reshape(count, 1, width) for value in (place_of, reach, back, spot))

    vmem = pl.BlockSpec(memory_space=pltpu.VMEM)
    dma = pltpu.SemaphoreType.DMA
    return pl.pallas_call(
        functools.partial(path_kernel, count, 1.0 / math.sqrt(VARS), 1.0 / math.sqrt(rows * count)),
        out_shape=(
            jax.ShapeDtypeStruct((columns, variants), F32),
            jax.ShapeDtypeStruct((columns, rows), BF16),
        ),
        in_specs=[pl.BlockSpec(memory_space=pl.ANY)] + [vmem] * 8,
        out_specs=(vmem, vmem),
        scratch_shapes=[
            pltpu.VMEM((rows, variants), BF16),
            pltpu.VMEM((rows, total), BF16),
            pltpu.VMEM((rows, total), BF16),
            pltpu.VMEM((rows, total), BF16),
            pltpu.VMEM((rows, total), BF16),
            pltpu.VMEM((columns // 2, rows), F32),
            pltpu.VMEM((columns // 2, rows), F32),
            pltpu.VMEM((columns // 2, rows), F32),
            pltpu.VMEM((count, 1, width), jnp.int32),
            pltpu.VMEM((count, 8, width), F32),
            pltpu.VMEM((count, 8, width), F32),
            pltpu.VMEM((count, columns, part), BF16),
            pltpu.VMEM((columns, part), F32),
            pltpu.VMEM((columns // 2, rows), F32),
            pltpu.VMEM((2, columns // 2, rows), F32),
            pltpu.VMEM((count, columns // 2, width), F32),
            pltpu.VMEM((count, columns // 2, width), F32),
            pltpu.VMEM((count, columns // 2, width), F32),
            pltpu.VMEM((count, columns // 2, width), F32),
            pltpu.VMEM((count, columns, part), BF16),
            pltpu.VMEM((count, columns, part), BF16),
            pltpu.VMEM((columns, rows), F32),
            pltpu.VMEM((columns // 2, rows), F32),
            dma, dma,
            dma,
        ] + [dma((count,))] * 4 + [dma((count, CUTS))] * 2 + [
            dma, dma((2,)),
        ] + [dma((count,))] * 6 + [dma((count, CUTS))] * 4,
        compiler_params=pltpu.CompilerParams(
            collective_id=0, has_side_effects=True, vmem_limit_bytes=60 * 1024 * 1024
        ),
    )(
        genotypes, coefficients, (fold_label * 2 + event_flag)[None], place_of, reach, back, spot,
        step_size[None], penalty[None],
    )


def solution(mesh):
    placed = (
        P("samp", "var"),
        P("pheno", "var"),
        P(("pheno", "samp")),
        P(("pheno", "samp")),
        P(("pheno", "samp")),
        P(),
        P(),
    )
    return jax.shard_map(
        local,
        mesh=mesh,
        in_specs=placed,
        out_specs=(P("pheno", "var"), P("pheno", "samp")),
        check_vma=False,
    )
```

```python
import functools
import math

import jax
import jax.numpy as jnp
from jax import lax
from jax.experimental import pallas as pl
from jax.experimental.pallas import tpu as pltpu
from jax.sharding import PartitionSpec as P

VARS = 16384
FOLDS = 8
ITERS = 3
MESH = pl.DeviceIdType.MESH
CUTS_LOW = 1
CUTS = 4
F32 = jnp.float32
BF16 = jnp.bfloat16


def each(count, body):
    if count <= 8:
        for step in range(count):
            body(step)
    else:
        lax.fori_loop(0, count, lambda step, carry: (body(step), carry)[1], 0)


def halves(value):
    high = value.astype(BF16)
    low = (value - high.astype(F32)).astype(BF16)
    return jnp.concatenate([high, low], axis=0)


def across(left, right):
    return lax.dot_general(left, right, (((1,), (1,)), ((), ())), preferred_element_type=F32)


def across2(value, matrix):
    rows = value.shape[0]
    both = across(halves(value), matrix)
    return both[:rows] + both[rows:]


def dot2(value, matrix):
    rows = value.shape[0]
    both = jnp.dot(halves(value), matrix, preferred_element_type=F32)
    return both[:rows] + both[rows:]


def path_kernel(
    count, scale_vars, scale_samples,
    geno_in, coef_in, code_row, place_out, reach, back, spot, step_row, penalty_row,
    coef_out, score_out,
    geno, to_time, later, earlier, to_id, mask, kept, kept_time, place_in, code_out, code_in,
    low, shard, half_send, half_recv, out_a, in_a, out_b, in_b, out_g, in_g, pred, held, s_ss, s_rs,
    load_sem, p_ss, p_rs, l_ss, l_rs, fwd_ss, last_ss, half_ss, half_rs, a_ss, a_rs, b_ss, b_rs, g_ss, g_rs, c_ss, c_rs, f_ss, f_rs,
):
    me = lax.axis_index("samp")
    var = lax.axis_index("var")
    columns, variants = coef_in.shape
    rows = geno.shape[0]
    part = variants // count
    width = later.shape[1] // count
    share = rows // count
    half = count // 2
    few = columns // 2
    mine = pl.ds(pl.multiple_of(var * few, few), few)
    theirs = pl.ds(pl.multiple_of((1 - var) * few, few), few)
    load = pltpu.make_async_copy(geno_in, geno, load_sem)
    load.start()

    def peer(step):
        return lax.rem(me + step, count)

    def piece(owner):
        return pl.ds(pl.multiple_of(owner * part, part), part)

    side = 1 - 2 * lax.rem(me, 2)

    def down(step):
        return lax.rem(me + 2 * step, count)

    cut = columns // CUTS
    cut_low = columns // CUTS_LOW

    def bit(owner, number):
        return low.at[owner, pl.ds(number * cut_low, cut_low), :]

    def wide(owner, number):
        return coef_out.at[pl.ds(number * cut, cut), piece(owner)]

    def send_to(spot_of, ssem, rsem, number, owner):
        return pltpu.make_async_remote_copy(
            src_ref=spot_of(me, number), dst_ref=spot_of(me, number),
            send_sem=ssem.at[owner, number], recv_sem=rsem.at[me, number],
            device_id={"samp": owner}, device_id_type=MESH,
        )

    def pass_on(spot_of, ssem, rsem, number, owner):
        return pltpu.make_async_remote_copy(
            src_ref=spot_of(owner, number), dst_ref=spot_of(owner, number),
            send_sem=ssem.at[owner, number], recv_sem=rsem.at[owner, number],
            device_id={"samp": me + side}, device_id_type=MESH,
        )

    def spread_out(spot_of, ssem, rsem):
        for number in range(CUTS_LOW if spot_of is bit else CUTS):
            def go(step):
                send_to(spot_of, ssem, rsem, number, down(step + 1)).start()
            send_to(spot_of, ssem, rsem, number, me + side).start()
            each(half - 1, go)

    def relay_all(spot_of, ssem, rsem):
        for number in range(CUTS_LOW if spot_of is bit else CUTS):
            def go(step):
                copy = pass_on(spot_of, ssem, rsem, number, down(step + 1))
                copy.wait_recv()
                copy.start()
            each(half - 1, go)

    def land(spot_of, ssem, rsem, owner):
        for number in range(CUTS_LOW if spot_of is bit else CUTS):
            pass_on(spot_of, ssem, rsem, number, owner).wait_recv()

    def settle(spot_of, ssem, fsem, rsem):
        for number in range(CUTS_LOW if spot_of is bit else CUTS):
            def go(step):
                owner = down(step + 1)
                send_to(spot_of, ssem, rsem, number, owner).wait_send()
                pass_on(spot_of, fsem, rsem, number, owner).wait_send()
            each(half - 1, go)
            send_to(spot_of, ssem, rsem, number, me + side).wait_send()

    def slots(owner):
        return pl.ds(pl.multiple_of(owner * width, width), width)

    barrier = pltpu.get_barrier_semaphore()

    def greet(step):
        pl.semaphore_signal(barrier, inc=1, device_id={"samp": peer(step + 1)}, device_id_type=MESH)

    each(count - 1, greet)
    pl.semaphore_signal(barrier, inc=1, device_id={"var": 1 - var}, device_id_type=MESH)
    pl.semaphore_wait(barrier, count)

    def send(source, target, ssem, rsem, owner):
        return pltpu.make_async_remote_copy(
            src_ref=source,
            dst_ref=target,
            send_sem=ssem.at[owner],
            recv_sem=rsem.at[me],
            device_id={"samp": owner},
            device_id_type=MESH,
        )

    def arrive(source, target, ssem, rsem, owner):
        pltpu.make_async_remote_copy(
            src_ref=source,
            dst_ref=target,
            send_sem=ssem.at[owner],
            recv_sem=rsem.at[owner],
            device_id={"samp": owner},
            device_id_type=MESH,
        ).wait_recv()

    def push_p(step):
        owner = peer(step + 1)
        send(place_out.at[owner], place_in.at[me], p_ss, p_rs, owner).start()
    each(count - 1, push_p)

    line = lax.broadcasted_iota(jnp.int32, (8, rows), 0)
    labels = jnp.where(line == 0, code_row[...] // 2, jnp.where(line == 1, code_row[...] % 2, 0)).astype(F32)
    same = lax.broadcasted_iota(jnp.int32, (columns, columns), 0) == lax.broadcasted_iota(
        jnp.int32, (columns, columns), 1
    )
    pace = jnp.sum(jnp.where(same, step_row[...], 0.0), axis=1, keepdims=True)
    threshold = pace * jnp.sum(jnp.where(same, penalty_row[...], 0.0), axis=1, keepdims=True)
    column_fold = lax.rem(lax.broadcasted_iota(jnp.int32, (few, rows), 0) + var * few, FOLDS).astype(F32)
    mask[...] = jnp.where(labels[0:1, :] != column_fold, 1.0, 0.0)
    kept[...] = mask[...] * labels[1:2, :]
    ranks = lax.broadcasted_iota(jnp.int32, (rows, width), 0)
    lane = lax.broadcasted_iota(jnp.int32, (rows, width), 1)
    for owner in range(count):
        span = slice(owner * width, (owner + 1) * width)
        later[:, span] = jnp.where(reach[owner] >= ranks, 1.0, 0.0).astype(BF16)
        earlier[:, span] = jnp.where(back[owner] >= ranks, 1.0, 0.0).astype(BF16)

    place_in[me] = place_out[me]
    block = jnp.zeros((rows, width), jnp.int32)
    def land_p(step):
        owner = peer(step + 1)
        arrive(place_out.at[owner], place_in.at[owner], p_ss, p_rs, owner)
        send(place_out.at[owner], place_in.at[me], p_ss, p_rs, owner).wait_send()
    each(count - 1, land_p)
    for owner in range(1, count):
        block += jnp.where(place_in[owner] == ranks, owner, 0)
    block = jnp.broadcast_to(jnp.sum(block, axis=1, keepdims=True), (rows, width))
    in_totals = (lane - share) == block
    for owner in range(count):
        span = slice(owner * width, (owner + 1) * width)
        hit = place_in[owner] == ranks
        to_time[:, span] = jnp.where(hit | in_totals, 1.0, 0.0).astype(BF16)
        to_id[:, span] = jnp.where(hit | ((lane == share) & (block > owner)), 1.0, 0.0).astype(BF16)
    spread = jnp.dot(labels.astype(BF16), to_time[...], preferred_element_type=F32)
    for owner in range(count):
        code_out[owner] = spread[:, owner * width:(owner + 1) * width]

    def push_l(step):
        owner = peer(step + 1)
        send(code_out.at[owner], code_in.at[me], l_ss, l_rs, owner).start()
    each(count - 1, push_l)
    code_in[me] = code_out[me]

    def land_l(step):
        owner = peer(step + 1)
        arrive(code_out.at[owner], code_in.at[owner], l_ss, l_rs, owner)
        send(code_out.at[owner], code_in.at[me], l_ss, l_rs, owner).wait_send()
    each(count - 1, land_l)
    labels_time = jnp.zeros((labels.shape[0], rows), F32)
    for owner in range(count):
        labels_time += across(
            code_in[owner].astype(BF16), jnp.where(spot[owner] == ranks, 1.0, 0.0).astype(BF16)
        )
    kept_time[...] = jnp.where(labels_time[0:1, :] != column_fold, 1.0, 0.0) * labels_time[1:2, :]

    def fill(step):
        low[step] = coef_in[:, piece(step)].astype(BF16)

    each(count, fill)
    shard[...] = coef_in[:, piece(me)]
    load.wait()

    def one_step(turn, carry):
        pred[...] = jnp.zeros_like(pred)

        def add_part(owner):
            pred[...] += across(low[owner], geno[:, piece(owner)])

        def add_down(step):
            add_part(down(step + 1))

        def add_side(step):
            owner = down(step) + side

            @pl.when(turn > 0)
            def _():
                land(bit, c_ss, c_rs, owner)
            add_part(owner)

        add_part(me)

        @pl.when(turn > 0)
        def _():
            relay_all(bit, fwd_ss, c_rs)
        each(half - 1, add_down)
        each(half, add_side)
        half_send[...] = pred[theirs, :]
        slot = lax.rem(turn, 2)
        swap = pltpu.make_async_remote_copy(
            src_ref=half_send, dst_ref=half_recv.at[slot], send_sem=half_ss, recv_sem=half_rs.at[slot],
            device_id={"var": 1 - var}, device_id_type=MESH,
        )
        swap.start()
        swap.wait()

        @pl.when(turn > 0)
        def _():
            settle(bit, c_ss, fwd_ss, c_rs)

        weight = mask[...] * jnp.exp((pred[mine, :] + half_recv[slot]) * scale_vars)
        held[...] = weight
        spread = dot2(weight, to_time[...])
        for owner in range(count):
            out_a[owner] = spread[:, owner * width:(owner + 1) * width]

        def push_a(step):
            owner = peer(step + 1)
            send(out_a.at[owner], in_a.at[me], a_ss, a_rs, owner).start()
        each(count - 1, push_a)
        risk = across2(out_a[me], later[:, slots(me)])
        for step in range(count - 1):
            owner = peer(step + 1)
            arrive(out_a.at[owner], in_a.at[owner], a_ss, a_rs, owner)
            risk += across2(in_a[owner], later[:, slots(owner)])
        events = kept_time[...]
        ratio = events / jnp.where(events > 0, risk, 1.0)
        spread = dot2(ratio, earlier[...])
        for owner in range(count):
            out_b[owner] = spread[:, owner * width:(owner + 1) * width]

        def push_b(step):
            owner = peer(step + 1)
            send(out_b.at[owner], in_b.at[me], b_ss, b_rs, owner).start()
        each(count - 1, push_b)
        hazard = across2(out_b[me], to_id[:, slots(me)])
        for step in range(count - 1):
            owner = peer(step + 1)
            arrive(out_b.at[owner], in_b.at[owner], b_ss, b_rs, owner)
            hazard += across2(in_b[owner], to_id[:, slots(owner)])
        score_out[mine, :] = (held[...] * hazard - kept[...]).astype(BF16)
        trade = pltpu.make_async_remote_copy(
            src_ref=score_out.at[mine, :], dst_ref=score_out.at[mine, :], send_sem=s_ss, recv_sem=s_rs,
            device_id={"var": 1 - var}, device_id_type=MESH,
        )
        trade.start()
        trade.wait()

        def push_g(step):
            owner = peer(step + 1)
            out_g[owner] = jnp.dot(
                score_out[...], geno[:, piece(owner)], preferred_element_type=F32
            ).astype(out_g.dtype)
            send(out_g.at[owner], in_g.at[me], g_ss, g_rs, owner).start()
        each(count - 1, push_g)
        total = jnp.dot(score_out[...], geno[:, piece(me)], preferred_element_type=F32)
        for step in range(count - 1):
            owner = peer(count - 1 - step)
            arrive(out_g.at[owner], in_g.at[owner], g_ss, g_rs, owner)
            total += in_g[owner].astype(F32)
        stepped = shard[...] - pace * (total * scale_samples)
        shrunk = jnp.maximum(jnp.abs(stepped) - threshold, 0.0)
        fresh = jnp.where(stepped > 0, shrunk, -shrunk)
        shard[...] = fresh

        def drained_all(step):
            owner = peer(step + 1)
            send(out_a.at[owner], in_a.at[me], a_ss, a_rs, owner).wait_send()
            send(out_b.at[owner], in_b.at[me], b_ss, b_rs, owner).wait_send()
            send(out_g.at[owner], in_g.at[me], g_ss, g_rs, owner).wait_send()

        @pl.when(turn < ITERS - 1)
        def _():
            low[me] = fresh.astype(BF16)

            spread_out(bit, c_ss, c_rs)

        each(count - 1, drained_all)
        return carry

    lax.fori_loop(0, ITERS, one_step, 0)

    coef_out[:, piece(me)] = shard[...]

    spread_out(wide, f_ss, f_rs)
    relay_all(wide, last_ss, f_rs)

    def land_f(step):
        land(wide, f_ss, f_rs, down(step) + side)
    each(half, land_f)
    settle(wide, f_ss, last_ss, f_rs)


def local(genotypes, coefficients, time_order, fold_label, event_flag, penalty, step_size):
    rows = genotypes.shape[0]
    columns, variants = coefficients.shape
    count = lax.axis_size("samp")
    me = lax.axis_index("samp")
    share = rows // count
    width = -(-(share + count) // 128) * 128
    total = count * width
    part = variants // count

    ranks = jnp.arange(rows, dtype=jnp.int32)
    slot_all = jnp.arange(total, dtype=jnp.int32)
    lane = slot_all % width
    owner = time_order // rows
    place = time_order % rows
    same = (owner[:, None] == owner[None, :]) & (ranks[:, None] < ranks[None, :])
    key = owner * width + jnp.sum(same.astype(jnp.int32), axis=0)
    match = key[:, None] == slot_all[None, :]
    rank_of = jnp.max(jnp.where(match, ranks[:, None], -1), axis=0)
    place_of = jnp.max(jnp.where(match, place[:, None], -1), axis=0)
    in_totals = (lane >= share) & (lane < share + count)
    spot = jnp.where(lane < share, rank_of, -1)
    reach = jnp.where(in_totals & (lane - share > me), rows, spot)
    back = jnp.where(lane == share, rows, spot)
    place_of, reach, back, spot = (value.reshape(count, 1, width) for value in (place_of, reach, back, spot))

    vmem = pl.BlockSpec(memory_space=pltpu.VMEM)
    dma = pltpu.SemaphoreType.DMA
    return pl.pallas_call(
        functools.partial(path_kernel, count, 1.0 / math.sqrt(VARS), 1.0 / math.sqrt(rows * count)),
        out_shape=(
            jax.ShapeDtypeStruct((columns, variants), F32),
            jax.ShapeDtypeStruct((columns, rows), BF16),
        ),
        in_specs=[pl.BlockSpec(memory_space=pl.ANY)] + [vmem] * 8,
        out_specs=(vmem, vmem),
        scratch_shapes=[
            pltpu.VMEM((rows, variants), BF16),
            pltpu.VMEM((rows, total), BF16),
            pltpu.VMEM((rows, total), BF16),
            pltpu.VMEM((rows, total), BF16),
            pltpu.VMEM((rows, total), BF16),
            pltpu.VMEM((columns // 2, rows), F32),
            pltpu.VMEM((columns // 2, rows), F32),
            pltpu.VMEM((columns // 2, rows), F32),
            pltpu.VMEM((count, 1, width), jnp.int32),
            pltpu.VMEM((count, 8, width), F32),
            pltpu.VMEM((count, 8, width), F32),
            pltpu.VMEM((count, columns, part), BF16),
            pltpu.VMEM((columns, part), F32),
            pltpu.VMEM((columns // 2, rows), F32),
            pltpu.VMEM((2, columns // 2, rows), F32),
            pltpu.VMEM((count, columns // 2, width), F32),
            pltpu.VMEM((count, columns // 2, width), F32),
            pltpu.VMEM((count, columns // 2, width), F32),
            pltpu.VMEM((count, columns // 2, width), F32),
            pltpu.VMEM((count, columns, part), BF16),
            pltpu.VMEM((count, columns, part), BF16),
            pltpu.VMEM((columns, rows), F32),
            pltpu.VMEM((columns // 2, rows), F32),
            dma, dma,
            dma,
        ] + [dma((count,))] * 4 + [dma((count, CUTS))] * 2 + [
            dma, dma((2,)),
        ] + [dma((count,))] * 6 + [dma((count, CUTS))] * 4,
        compiler_params=pltpu.CompilerParams(
            collective_id=0, has_side_effects=True, vmem_limit_bytes=60 * 1024 * 1024
        ),
    )(
        genotypes, coefficients, (fold_label * 2 + event_flag)[None], place_of, reach, back, spot,
        step_size[None], penalty[None],
    )


def solution(mesh):
    placed = (
        P("samp", "var"),
        P("pheno", "var"),
        P(("pheno", "samp")),
        P(("pheno", "samp")),
        P(("pheno", "samp")),
        P(),
        P(),
    )
    return jax.shard_map(
        local,
        mesh=mesh,
        in_specs=placed,
        out_specs=(P("pheno", "var"), P("pheno", "samp")),
        check_vma=False,
    )
```
